32 devices in a mesh: section: 2 (over x), rep: 2 (over core), fsdp: 8 (over z, y).
Axes of the slice: x: 2, y: 2, z: 4, core: 2. Of those that a mesh axis runs over, the one named last changes fastest.
Arguments:
- inputs: float32 [2, 2048, 2048], P(None, ('rep', 'fsdp')), may hold values from -6 to 6
- segments: int32 [2, 2048], P(None, ('rep', 'fsdp')), may hold values from 0 to 127, as said below
- cotangent: float32 [2, 2048, 2048], P(None, ('rep', 'fsdp')), may hold values from -6 to 6
- w_qkv: bfloat16 [2, 6144, 2048], P('section', 'fsdp'), may hold values from -0.125 to 0.125
- b_qkv: bfloat16 [2, 6144], P('section', 'fsdp'), may hold values from -9.5 to 9.5
- w_dense: bfloat16 [2, 2048, 2048], P('section', 'fsdp'), may hold values from -0.5 to 0.5
- b_dense: bfloat16 [2, 2048], P('section', 'fsdp'), may hold values from -3 to 3
- w_up: bfloat16 [2, 8192, 2048], P('section', 'fsdp'), may hold values from -0.125 to 0.125
- b_up: bfloat16 [2, 8192], P('section', 'fsdp'), may hold values from -3 to 3
- w_down: bfloat16 [2, 2048, 8192], P('section', 'fsdp'), may hold values from -0.125 to 0.125
- b_down: bfloat16 [2, 2048], P('section', 'fsdp'), may hold values from -3 to 3
- layer_norm_gain: bfloat16 [2, 2048], P('section', 'fsdp'), may hold values from 0.5 to 1.5
- ln_bias: bfloat16 [2, 2048], P('section', 'fsdp'), may hold values from -3 to 3
Outputs:
- layer_out: float32 [2, 2, 2048, 2048], P('section', None, ('rep', 'fsdp'))
- input_grad: float32 [2, 2, 2048, 2048], P('section', None, ('rep', 'fsdp'))
- g_w_qkv: float32 [2, 6144, 2048], P('section', 'fsdp')
- g_b_qkv: float32 [2, 6144], P('section', 'fsdp')
- g_w_dense: float32 [2, 2048, 2048], P('section', 'fsdp')
- g_b_dense: float32 [2, 2048], P('section', 'fsdp')
- g_w_up: float32 [2, 8192, 2048], P('section', 'fsdp')
- g_b_up: float32 [2, 8192], P('section', 'fsdp')
- g_w_down: float32 [2, 2048, 8192], P('section', 'fsdp')
- g_b_down: float32 [2, 2048], P('section', 'fsdp')
- g_ln_gain: float32 [2, 2048], P('section', 'fsdp')
- g_ln_bias: float32 [2, 2048], P('section', 'fsdp')
The draws below stay inside these ranges and needn't reach their ends.
Inputs may be any that keep to these rules, and one draw needn't show every extreme that they name: `segments`: every aligned block of 128 tokens of a micro-batch begins a new sequence at its first token; within a block ids count the sequences from 0 and never fall.
All inputs are finite; a program needn't handle non-finite values.
Results may differ from the reference program's by a relative error of at most 0.025.
The reference program's roundings to bfloat16 on the way count: a program that leaves them out, or rounds other values in their place, can miss the bound.
Values may be sent and summed in bfloat16 or wider, within the bound.
No kernel may reach another device: no remote copies, remote signals or barrier semaphores. Data moves between devices by JAX's collectives and lax.ppermute only.
A program may use at most 640 MiB of HBM per device.

```python
import jax
import jax.numpy as jnp
from jax import lax

D = 2048
FF = 8192
ROWS = 128
MICRO = 2
TOKENS = 2048
LAYERS = 2


def draw_segments(key, part):
    fresh = jax.random.randint(key, (MICRO, TOKENS), 0, 256)
    block_count = TOKENS // ROWS
    chosen = jax.random.randint(jax.random.fold_in(key, 7), (MICRO,), 0, block_count)
    block_of = jnp.arange(TOKENS) // ROWS
    singles = block_of[None, :] == chosen[:, None]
    block_starts = jnp.arange(TOKENS) % ROWS == 0
    starts = ((fresh == 0) | block_starts[None, :] | singles).astype(jnp.int32)
    blocked = starts.reshape(MICRO, block_count, ROWS)
    counted = jnp.cumsum(blocked, axis=2) - 1
    return counted.reshape(MICRO, TOKENS).astype(jnp.int32)


def draw_b_qkv(key, part):
    values = jnp.clip(0.5 * jax.random.normal(key, (LAYERS, 3 * D), jnp.float32), -3.0, 3.0)
    return values.astype(jnp.bfloat16)


def levels(own_key, extent, cuts, smallest, largest):
    loudness = 1.0
    for axis_at, blocks in cuts:
        heights = jax.random.uniform(jax.random.fold_in(jax.random.fold_in(own_key, 6), axis_at), (blocks,), jnp.float32, smallest / len(cuts), largest / len(cuts))
        loudness = loudness * jnp.repeat(jnp.exp(heights), extent[axis_at] // blocks).reshape((-1,) + (1,) * (len(extent) - 1 - axis_at))
    return loudness


def bell_draw(stream_key, dims, spread, most, cuts=(), dtype=jnp.bfloat16):
    values = spread * jax.random.normal(stream_key, dims, jnp.float32)
    if cuts:
        values = values * levels(stream_key, dims, cuts, -0.22, 0.18)
    return jnp.clip(values, -most, most).astype(dtype)


def setup_inputs(seed: int = 0) -> dict:
    streams_of = jax.random.split(jax.random.key(seed), 14)
    return {
        "inputs": bell_draw(streams_of[0], (MICRO, TOKENS, D), 1.0, 6.0, ((1, 16),), jnp.float32),
        "segments": draw_segments(jax.random.fold_in(streams_of[13], 71), 0),
        "cotangent": bell_draw(streams_of[2], (MICRO, TOKENS, D), 1.0, 6.0, ((1, 16),), jnp.float32),
        "w_qkv": bell_draw(streams_of[3], (LAYERS, 3 * D, D), D ** -0.5, 0.125, ((0, 2), (1, 8))),
        "b_qkv": draw_b_qkv(jax.random.fold_in(streams_of[13], 71), 0),
        "w_dense": bell_draw(streams_of[5], (LAYERS, D, D), (D // 16) ** -0.5, 0.5, ((0, 2), (1, 8))),
        "b_dense": bell_draw(streams_of[6], (LAYERS, D), 0.5, 3.0, ((0, 2), (1, 8))),
        "w_up": bell_draw(streams_of[7], (LAYERS, FF, D), D ** -0.5, 0.125, ((0, 2), (1, 8))),
        "b_up": bell_draw(streams_of[8], (LAYERS, FF), 0.5, 3.0, ((0, 2), (1, 8))),
        "w_down": bell_draw(streams_of[9], (LAYERS, D, FF), (FF // 4) ** -0.5, 0.125, ((0, 2), (1, 8))),
        "b_down": bell_draw(streams_of[10], (LAYERS, D), 0.5, 3.0, ((0, 2), (1, 8))),
        "layer_norm_gain": jnp.clip(1.0 + 0.1 * jax.random.normal(streams_of[11], (LAYERS, D), jnp.float32), 0.5, 1.5).astype(jnp.bfloat16),
        "ln_bias": bell_draw(streams_of[12], (LAYERS, D), 0.5, 3.0, ((0, 2), (1, 8))),
    }


EPSILON = 1e-05
GELU_SCALE = 0.7978845608028654
GELU_CUBIC = 0.044715
NEG_FILL = -1e+30

def matmul_rows(left_arr, right_arr):
    return jnp.dot(left_arr, right_arr, preferred_element_type=jnp.float32)

def batched(form, left_arr, right_arr):
    return jnp.einsum(form, left_arr.astype(jnp.float32), right_arr.astype(jnp.float32))

def block_tables(seg_blocks):
    length = seg_blocks.shape[1]
    places = jnp.arange(length)
    earlier = places[None, :] <= places[:, None]
    strict = places[None, :] < places[:, None]
    same_seq = seg_blocks[:, :, None] == seg_blocks[:, None, :]
    allowed = same_seq & earlier[None]
    offsets = lax.optimization_barrier(jnp.sum(jnp.where(same_seq & strict[None], 1.0, 0.0).astype(jnp.float32), axis=2))
    frequencies = jnp.power(10000.0, -jnp.arange(16).astype(jnp.float32) / 16.0).astype(jnp.float32)
    angles = offsets[:, :, None] * frequencies
    return (allowed, jnp.cos(angles), jnp.sin(angles))

def rotate(tensor, cosine_table, sine_table, direction):
    first_half = tensor[..., :16]
    second_half = tensor[..., 16:32]
    cos_b = cosine_table[:, :, None, :]
    sin_b = sine_table[:, :, None, :] * direction
    return jnp.concatenate([first_half * cos_b - second_half * sin_b, second_half * cos_b + first_half * sin_b, tensor[..., 32:]], axis=-1)

def gelu_value(pre_act):
    inner_arg = GELU_SCALE * (pre_act + GELU_CUBIC * pre_act * pre_act * pre_act)
    return 0.5 * pre_act * (1.0 + jnp.tanh(inner_arg))

def gelu_slope(pre_act):
    inner_arg = GELU_SCALE * (pre_act + GELU_CUBIC * pre_act * pre_act * pre_act)
    tangent = jnp.tanh(inner_arg)
    return 0.5 * (1.0 + tangent) + 0.5 * pre_act * (1.0 - tangent * tangent) * GELU_SCALE * (1.0 + 3.0 * GELU_CUBIC * pre_act * pre_act)

def masked_scores(query_rows, key_rows, allowed):
    scores = batched('bqhd,bkhd->bhqk', query_rows, key_rows) * 0.125
    return jnp.where(allowed[:, None], scores, NEG_FILL)

def layer_forward(layer_in, seg_blocks, w_qkv, b_qkv, w_dense, b_dense, w_up, b_up, w_down, b_down, layer_norm_gain, ln_bias):
    row_total, model_width = layer_in.shape
    block_count, length = seg_blocks.shape
    head_count = model_width // 64
    allowed, cosine_table, sine_table = block_tables(seg_blocks)
    average = lax.optimization_barrier(jnp.mean(layer_in, axis=1, keepdims=True))
    centred = layer_in - average
    inverse_deviation = lax.rsqrt(lax.optimization_barrier(jnp.mean(centred * centred, axis=1, keepdims=True)) + EPSILON)
    standardized_input = centred * inverse_deviation
    normed = (standardized_input * layer_norm_gain.astype(jnp.float32) + ln_bias.astype(jnp.float32)).astype(jnp.bfloat16)
    projected = matmul_rows(normed, w_qkv.T) + b_qkv.astype(jnp.float32)
    shaped = projected.reshape(block_count, length, 3, head_count, 64)
    query_rows = rotate(shaped[:, :, 0], cosine_table, sine_table, 1.0).astype(jnp.bfloat16)
    key_rows = rotate(shaped[:, :, 1], cosine_table, sine_table, 1.0).astype(jnp.bfloat16)
    value_rows = shaped[:, :, 2].astype(jnp.bfloat16)
    scores = masked_scores(query_rows, key_rows, allowed)
    row_max = lax.optimization_barrier(jnp.max(scores, axis=3, keepdims=True))
    log_total = row_max + jnp.log(lax.optimization_barrier(jnp.sum(jnp.exp(scores - row_max), axis=3, keepdims=True)))
    attn_probs = jnp.exp(scores - log_total).astype(jnp.bfloat16)
    mixed_rows = batched('bhqk,bkhd->bqhd', attn_probs, value_rows).astype(jnp.bfloat16).reshape(row_total, model_width)
    attn_part = matmul_rows(mixed_rows, w_dense.T) + b_dense.astype(jnp.float32)
    up_input = matmul_rows(normed, w_up.T) + b_up.astype(jnp.float32)
    hidden = gelu_value(up_input).astype(jnp.bfloat16)
    down_part = matmul_rows(hidden, w_down.T) + b_down.astype(jnp.float32)
    result = layer_in + attn_part + down_part
    stored = (standardized_input, inverse_deviation, normed, query_rows, key_rows, value_rows, log_total, mixed_rows, up_input, hidden)
    return (result, stored)

def layer_backward(output_gradient, seg_blocks, stored, w_qkv, w_dense, w_up, w_down, layer_norm_gain):
    standardized_input, inverse_deviation, normed, query_rows, key_rows, value_rows, log_total, mixed_rows, up_input, hidden = stored
    row_total, model_width = output_gradient.shape
    block_count, length = seg_blocks.shape
    head_count = model_width // 64
    allowed, cosine_table, sine_table = block_tables(seg_blocks)
    grad_low = output_gradient.astype(jnp.bfloat16)
    d_hidden = matmul_rows(grad_low, w_down)
    d_up = d_hidden * gelu_slope(up_input)
    d_up_low = d_up.astype(jnp.bfloat16)
    d_mixed = matmul_rows(grad_low, w_dense).astype(jnp.bfloat16).reshape(block_count, length, head_count, 64)
    scores = masked_scores(query_rows, key_rows, allowed)
    attn_probs = jnp.exp(scores - log_total)
    probs_low = attn_probs.astype(jnp.bfloat16)
    d_probs = batched('bqhd,bkhd->bhqk', d_mixed, value_rows)
    d_values = batched('bhqk,bqhd->bkhd', probs_low, d_mixed)
    row_dot = lax.optimization_barrier(jnp.sum(attn_probs * d_probs, axis=3, keepdims=True))
    d_scores = (attn_probs * (d_probs - row_dot) * 0.125).astype(jnp.bfloat16)
    d_query = rotate(batched('bhqk,bkhd->bqhd', d_scores, key_rows), cosine_table, sine_table, -1.0)
    d_keys = rotate(batched('bhqk,bqhd->bkhd', d_scores, query_rows), cosine_table, sine_table, -1.0)
    d_proj = jnp.stack([d_query, d_keys, d_values], axis=2).reshape(row_total, 3 * model_width)
    d_proj_low = d_proj.astype(jnp.bfloat16)
    normalized_gradient = matmul_rows(d_up_low, w_up) + matmul_rows(d_proj_low, w_qkv)
    standardized_gradient = normalized_gradient * layer_norm_gain.astype(jnp.float32)
    input_gradient = output_gradient + inverse_deviation * (standardized_gradient - lax.optimization_barrier(jnp.mean(standardized_gradient, axis=1, keepdims=True)) - standardized_input * lax.optimization_barrier(jnp.mean(standardized_gradient * standardized_input, axis=1, keepdims=True)))
    products = (d_proj_low, normed, grad_low, mixed_rows, d_up_low, hidden)
    vectors = (lax.optimization_barrier(jnp.sum(d_proj, axis=0)), lax.optimization_barrier(jnp.sum(output_gradient, axis=0)), lax.optimization_barrier(jnp.sum(d_up, axis=0)), lax.optimization_barrier(jnp.sum(output_gradient, axis=0)), lax.optimization_barrier(jnp.sum(normalized_gradient * standardized_input, axis=0)), lax.optimization_barrier(jnp.sum(normalized_gradient, axis=0)))
    return (input_gradient, products, vectors)

def weight_grads(products):
    d_proj_low, normed, grad_low, mixed_rows, d_up_low, hidden = products
    return (matmul_rows(d_proj_low.T, normed), matmul_rows(grad_low.T, mixed_rows), matmul_rows(d_up_low.T, normed), matmul_rows(grad_low.T, hidden))

def reference(inputs, segments, cotangent, w_qkv, b_qkv, w_dense, b_dense, w_up, b_up, w_down, b_down, layer_norm_gain, ln_bias):
    every = (w_qkv, b_qkv, w_dense, b_dense, w_up, b_up, w_down, b_down, layer_norm_gain, ln_bias)
    layer_params = [tuple((member[layer_index] for member in every)) for layer_index in range(2)]
    outputs = [[], []]
    input_grads = [[], []]
    totals = [None, None]
    for micro_index in range(MICRO):
        seg_blocks = segments[micro_index].reshape(-1, ROWS)
        current = inputs[micro_index]
        stored = []
        for layer_index in range(2):
            current, cache_now = layer_forward(current, seg_blocks, *layer_params[layer_index])
            outputs[layer_index].append(current)
            stored.append(cache_now)
        upstream = cotangent[micro_index]
        for layer_index in (1, 0):
            chosen = layer_params[layer_index]
            upstream_next, products, vectors = layer_backward(upstream, seg_blocks, stored[layer_index], chosen[0], chosen[2], chosen[4], chosen[6], chosen[8])
            input_grads[layer_index].append(upstream_next)
            matrices = weight_grads(products)
            terms = (matrices[0], vectors[0], matrices[1], vectors[1], matrices[2], vectors[2], matrices[3], vectors[3], vectors[4], vectors[5])
            if totals[layer_index] is None:
                totals[layer_index] = terms
            else:
                totals[layer_index] = tuple((former + latter for former, latter in zip(totals[layer_index], terms)))
            upstream = upstream_next
    layer_out = jnp.stack([jnp.stack(outputs[0]), jnp.stack(outputs[1])])
    input_grad = jnp.stack([jnp.stack(input_grads[0]), jnp.stack(input_grads[1])])
    stacked = tuple((jnp.stack([totals[0][position], totals[1][position]]) for position in range(10)))
    return (layer_out, input_grad, stacked[0], stacked[1], stacked[2], stacked[3], stacked[4], stacked[5], stacked[6], stacked[7], stacked[8], stacked[9])
```

```python
import jax
import jax.numpy as jnp
from jax import lax
from jax.sharding import PartitionSpec as P

EPSILON = 1e-05
GELU_SCALE = 0.7978845608028654
GELU_CUBIC = 0.044715
NEG_FILL = -1e30
HEAD = 64
F32 = jnp.float32
BF16 = jnp.bfloat16


def dot_f32(form, left_arr, right_arr):
    return jnp.einsum(form, left_arr, right_arr, preferred_element_type=F32)


def ring_order(count):
    half = count // 2
    return [2 * place for place in range(half)] + [
        2 * (count - 1 - place) + 1 for place in range(half, count)
    ]


def ring_step(value, direction):
    count = lax.axis_size("fsdp")
    order = ring_order(count)
    pairs = [(order[place], order[(place + direction) % count]) for place in range(count)]
    return lax.ppermute(value, "fsdp", pairs)


def swap(value, axis):
    return lax.ppermute(value, axis, [(0, 1), (1, 0)])


def one_way(value, axis, source):
    return lax.ppermute(value, axis, [(source, 1 - source)])


def ring_gather(block):
    half = lax.axis_size("fsdp") // 2
    middle = block.shape[1] // 2
    blocks = {0: block}
    behind = ahead = block
    for step in range(1, half):
        behind = ring_step(behind, 1)
        ahead = ring_step(ahead, -1)
        blocks[-step] = behind
        blocks[step] = ahead
    left = ring_step(behind[:, :middle], 1)
    right = ring_step(ahead[:, middle:], -1)
    blocks[half] = jnp.concatenate([left, right], axis=1)
    return blocks


def ring_scatter(parts):
    half = lax.axis_size("fsdp") // 2
    middle = parts[0].shape[1] // 2
    upward = parts[half][:, :middle].astype(BF16)
    downward = parts[half][:, middle:].astype(BF16)
    for step in range(half - 1, 0, -1):
        upward = ring_step(upward, 1).astype(F32)
        downward = ring_step(downward, -1).astype(F32)
        plus, minus = parts[step].astype(F32), parts[-step].astype(F32)
        if step == half - 1:
            upward = jnp.concatenate([plus[:, :middle] + upward, plus[:, middle:]], axis=1)
            downward = jnp.concatenate([minus[:, :middle], minus[:, middle:] + downward], axis=1)
        else:
            upward = plus + upward
            downward = minus + downward
        upward = upward.astype(BF16)
        downward = downward.astype(BF16)
    upward = ring_step(upward, 1).astype(F32)
    downward = ring_step(downward, -1).astype(F32)
    if half == 1:
        return parts[0].astype(F32) + jnp.concatenate([upward, downward], axis=1)
    return parts[0].astype(F32) + upward + downward


def exchange(chunks):
    return lax.all_to_all(chunks, "fsdp", 0, 0, tiled=False)


def block_tables(seg_blocks):
    length = seg_blocks.shape[1]
    places = jnp.arange(length)
    earlier = places[None, :] <= places[:, None]
    strict = places[None, :] < places[:, None]
    same_seq = seg_blocks[:, :, None] == seg_blocks[:, None, :]
    allowed = same_seq & earlier[None]
    offsets = jnp.sum(jnp.where(same_seq & strict[None], 1.0, 0.0).astype(F32), axis=2)
    frequencies = jnp.power(10000.0, -jnp.arange(16).astype(F32) / 16.0)
    angles = offsets[:, :, None] * frequencies
    return (allowed, jnp.cos(angles), jnp.sin(angles))


def rotate(tensor, cosine_table, sine_table, direction):
    first_half = tensor[..., :16]
    second_half = tensor[..., 16:32]
    cos_b = cosine_table[:, :, None, :]
    sin_b = sine_table[:, :, None, :] * direction
    return jnp.concatenate(
        [
            first_half * cos_b - second_half * sin_b,
            second_half * cos_b + first_half * sin_b,
            tensor[..., 32:],
        ],
        axis=-1,
    )


def gelu_value(pre_act):
    inner_arg = GELU_SCALE * (pre_act + GELU_CUBIC * pre_act * pre_act * pre_act)
    return 0.5 * pre_act * (1.0 + jnp.tanh(inner_arg))


def gelu_slope(pre_act):
    inner_arg = GELU_SCALE * (pre_act + GELU_CUBIC * pre_act * pre_act * pre_act)
    tangent = jnp.tanh(inner_arg)
    return 0.5 * (1.0 + tangent) + 0.5 * pre_act * (1.0 - tangent * tangent) * GELU_SCALE * (
        1.0 + 3.0 * GELU_CUBIC * pre_act * pre_act
    )


def masked_scores(query_rows, key_rows, allowed):
    scores = dot_f32("bqhd,bkhd->bhqk", query_rows, key_rows) * 0.125
    return jnp.where(allowed[:, None], scores, NEG_FILL)


def normalise(layer_in, gain, bias):
    average = jnp.mean(layer_in, axis=1, keepdims=True)
    centred = layer_in - average
    inverse_deviation = lax.rsqrt(jnp.mean(centred * centred, axis=1, keepdims=True) + EPSILON)
    standardized = centred * inverse_deviation
    normed = (standardized * gain + bias).astype(BF16)
    return standardized, inverse_deviation, normed


def group_forward(normed, tables, w_in, b_in, w_out):
    allowed, cosine_table, sine_table = tables
    block_count, length = cosine_table.shape[:2]
    row_count = normed.shape[0]
    units = w_in.shape[0] - w_out.shape[1]
    mixed_width = units // 2
    qkv_width = 3 * mixed_width
    heads = mixed_width // HEAD
    joint = dot_f32("td,od->to", normed, w_in) + b_in
    shaped = joint[:, :qkv_width].reshape(block_count, length, 3, heads, HEAD)
    up_input = joint[:, qkv_width:]
    query_rows = rotate(shaped[:, :, 0], cosine_table, sine_table, 1.0).astype(BF16)
    key_rows = rotate(shaped[:, :, 1], cosine_table, sine_table, 1.0).astype(BF16)
    value_rows = shaped[:, :, 2].astype(BF16)
    scores = masked_scores(query_rows, key_rows, allowed)
    row_max = jnp.max(scores, axis=3, keepdims=True)
    log_total = row_max + jnp.log(jnp.sum(jnp.exp(scores - row_max), axis=3, keepdims=True))
    attn_probs = jnp.exp(scores - log_total).astype(BF16)
    mixed_rows = (
        dot_f32("bhqk,bkhd->bqhd", attn_probs, value_rows)
        .astype(BF16)
        .reshape(row_count, mixed_width)
    )
    hidden = gelu_value(up_input).astype(BF16)
    features = jnp.concatenate([mixed_rows, hidden], axis=1)
    part = dot_f32("tf,of->to", features, w_out).astype(BF16)
    return part, (query_rows, key_rows, value_rows, log_total, up_input, features)


def group_backward(grad_low, tables, kept, w_in, w_out):
    allowed, cosine_table, sine_table = tables
    query_rows, key_rows, value_rows, log_total, up_input, features = kept
    block_count, length, heads = query_rows.shape[:3]
    row_count = grad_low.shape[0]
    mixed_width = heads * HEAD
    d_features = dot_f32("to,of->tf", grad_low, w_out)
    d_up = d_features[:, mixed_width:] * gelu_slope(up_input)
    d_mixed = d_features[:, :mixed_width].astype(BF16).reshape(block_count, length, heads, HEAD)
    scores = masked_scores(query_rows, key_rows, allowed)
    attn_probs = jnp.exp(scores - log_total)
    probs_low = attn_probs.astype(BF16)
    d_probs = dot_f32("bqhd,bkhd->bhqk", d_mixed, value_rows)
    d_values = dot_f32("bhqk,bqhd->bkhd", probs_low, d_mixed)
    row_dot = jnp.sum(attn_probs * d_probs, axis=3, keepdims=True)
    d_scores = (attn_probs * (d_probs - row_dot) * 0.125).astype(BF16)
    d_query = rotate(dot_f32("bhqk,bkhd->bqhd", d_scores, key_rows), cosine_table, sine_table, -1.0)
    d_keys = rotate(dot_f32("bhqk,bqhd->bkhd", d_scores, query_rows), cosine_table, sine_table, -1.0)
    d_proj = jnp.stack([d_query, d_keys, d_values], axis=2).reshape(row_count, 3 * mixed_width)
    d_joint = jnp.concatenate([d_proj, d_up], axis=1)
    d_joint_low = d_joint.astype(BF16)
    part = dot_f32("to,od->td", d_joint_low, w_in).astype(BF16)
    return part, d_joint_low, jnp.sum(d_joint, axis=0)


def distances(count):
    half = count // 2
    return [(step, -step) for step in range(1, half)] + [(0, half)]


def layer_forward(layer_in, tables, layer):
    standardized, inverse_deviation, normed = normalise(layer_in, layer["gain"], layer["bias"])
    blocks = ring_gather(normed)
    parts, kept, gathered = {}, [], []
    for group, table in zip(distances(lax.axis_size("fsdp")), tables):
        rows = jnp.concatenate([blocks[place] for place in group], axis=0)
        part, cache = group_forward(rows, table, layer["w_in"], layer["b_in"], layer["w_out"])
        length = layer_in.shape[0]
        for position, place in enumerate(group):
            parts[place] = part[position * length : (position + 1) * length]
        kept.append(cache)
        gathered.append(rows)
    result = layer_in + ring_scatter(parts) + layer["b_sum"]
    return result, (standardized, inverse_deviation, gathered, kept)


def layer_backward(grad, tables, stored, layer):
    standardized, inverse_deviation, gathered, kept = stored
    blocks = ring_gather(grad.astype(BF16))
    length = grad.shape[0]
    parts, d_joints, grads_low, sums = {}, [], [], 0.0
    for group, table, cache in zip(distances(lax.axis_size("fsdp")), tables, kept):
        rows = jnp.concatenate([blocks[place] for place in group], axis=0)
        part, d_joint_low, column_sum = group_backward(
            rows, table, cache, layer["w_in"], layer["w_out"]
        )
        for position, place in enumerate(group):
            parts[place] = part[position * length : (position + 1) * length]
        d_joints.append(d_joint_low)
        grads_low.append(rows)
        sums = sums + column_sum
    normalized_gradient = ring_scatter(parts)
    standardized_gradient = normalized_gradient * layer["gain"]
    input_gradient = grad + inverse_deviation * (
        standardized_gradient
        - jnp.mean(standardized_gradient, axis=1, keepdims=True)
        - standardized * jnp.mean(standardized_gradient * standardized, axis=1, keepdims=True)
    )
    g_out = dot_f32(
        "to,tf->of",
        jnp.concatenate(grads_low, axis=0),
        jnp.concatenate([cache[5] for cache in kept], axis=0),
    )
    g_in = dot_f32("to,td->od", jnp.concatenate(d_joints, axis=0), jnp.concatenate(gathered, axis=0))
    token_sums = jnp.stack(
        [
            jnp.sum(grad, axis=0),
            jnp.sum(normalized_gradient * standardized, axis=0),
            jnp.sum(normalized_gradient, axis=0),
        ]
    )
    return input_gradient, g_in.astype(BF16), g_out.astype(BF16), sums, token_sums


def unit_routes(count):
    routes, arrives = [], []
    for own in range(3):
        routes.append([(place, (3 * place + own) % count) for place in range(count)])
    for target in range(count):
        row = []
        for kind in range(3):
            row.append((kind * count + target) % 3)
        arrives.append(row)
    return routes, arrives


def table_row(table, axis):
    return jnp.asarray(table, jnp.int32)[lax.axis_index(axis)]


def pick_three(arrays, choice):
    stacked = jnp.stack(arrays)
    return jnp.stack([lax.dynamic_index_in_dim(stacked, choice[kind], 0, False) for kind in range(3)])


def units_to_heads(units):
    routes, arrives = unit_routes(lax.axis_size("fsdp"))
    moved = [lax.ppermute(units[own], "fsdp", routes[own]) for own in range(3)]
    return pick_three(moved, table_row(arrives, "fsdp"))


def heads_to_units(heads):
    routes, arrives = unit_routes(lax.axis_size("fsdp"))
    inverse = [[row.index(own) for own in range(3)] for row in arrives]
    leaving = pick_three([heads[kind] for kind in range(3)], table_row(inverse, "fsdp"))
    return jnp.stack(
        [
            lax.ppermute(leaving[own], "fsdp", [(target, source) for source, target in routes[own]])
            for own in range(3)
        ]
    )


def halves(mine, theirs, second_core, axis):
    return jnp.where(
        second_core,
        jnp.concatenate([theirs, mine], axis=axis),
        jnp.concatenate([mine, theirs], axis=axis),
    )


def shards(
    inputs,
    segments,
    cotangent,
    w_qkv,
    b_qkv,
    w_dense,
    b_dense,
    w_up,
    b_up,
    w_down,
    b_down,
    layer_norm_gain,
    ln_bias,
):
    section = lax.axis_index("section")
    core = lax.axis_index("rep")
    place = lax.axis_index("fsdp")
    count = lax.axis_size("fsdp")
    first_plane = section == 0
    second_core = core == 1
    length, width = inputs.shape[1:]
    unit = w_qkv.shape[1] // 3
    up_units = w_up.shape[1]
    out_rows = w_down.shape[1]
    features = unit + up_units
    half_unit, half_up, half_out = unit // 2, up_units // 2, out_rows // 2

    def by_plane(own, other):
        return (jnp.where(first_plane, own, other), jnp.where(first_plane, other, own))

    seg_own = lax.dynamic_index_in_dim(segments, section, 0, False)
    packed = jnp.concatenate(
        [
            b_dense[0],
            b_down[0],
            layer_norm_gain[0],
            ln_bias[0],
            b_qkv[0],
            b_up[0],
            seg_own.astype(BF16),
        ]
    )
    small = lax.all_gather(packed, ("section", "fsdp"), axis=0, tiled=False)
    small = small.reshape(2, count, -1).astype(F32)
    cuts = [0]
    for size in (out_rows, out_rows, out_rows, out_rows, 3 * unit, up_units, length):
        cuts.append(cuts[-1] + size)

    def vector(layer, number):
        return small[layer, :, cuts[number] : cuts[number + 1]].reshape(-1)

    def bias_in(layer):
        qkv = vector(layer, 4).reshape(3, count, unit)
        own_qkv = lax.dynamic_index_in_dim(qkv, place, 1, False).reshape(-1)
        own_up = lax.dynamic_index_in_dim(
            vector(layer, 5).reshape(count, up_units), place, 0, False
        )
        return jnp.concatenate([own_qkv, own_up])

    core_qkv = lax.dynamic_slice_in_dim(
        w_qkv[0].reshape(3, unit, width), core * half_unit, half_unit, 1
    )
    core_qkv = units_to_heads(core_qkv).reshape(3 * half_unit, width)
    core_up = lax.dynamic_slice_in_dim(w_up[0], core * half_up, half_up, 0)
    dense_rows = lax.dynamic_slice_in_dim(w_dense[0], core * half_out, half_out, 0)
    down_rows = lax.dynamic_slice_in_dim(w_down[0], core * half_out, half_out, 0)
    core_out = jnp.concatenate(
        [
            dense_rows.reshape(half_out, count, unit).transpose(1, 0, 2),
            down_rows.reshape(half_out, count, up_units).transpose(1, 0, 2),
        ],
        axis=2,
    )
    core_out = exchange(core_out)
    half_qkv = by_plane(core_qkv, swap(core_qkv, "section"))
    half_ups = by_plane(core_up, swap(core_up, "section"))
    half_outs = by_plane(core_out, swap(core_out, "section"))
    layers = []
    for layer in range(2):
        qkv_full = halves(
            half_qkv[layer].reshape(3, half_unit, width),
            swap(half_qkv[layer], "rep").reshape(3, half_unit, width),
            second_core,
            1,
        ).reshape(3 * unit, width)
        up_full = halves(half_ups[layer], swap(half_ups[layer], "rep"), second_core, 0)
        out_full = halves(half_outs[layer], swap(half_outs[layer], "rep"), second_core, 1)
        layers.append(
            {
                "w_in": jnp.concatenate([qkv_full, up_full], axis=0),
                "w_out": out_full.reshape(count * out_rows, features),
                "b_in": bias_in(layer),
                "b_sum": vector(layer, 0) + vector(layer, 1),
                "gain": vector(layer, 2),
                "bias": vector(layer, 3),
            }
        )

    order = ring_order(count)
    at = {device: spot for spot, device in enumerate(order)}
    groups = distances(count)
    table = [
        [order[(at[device] + step) % count] for group in groups for step in group]
        for device in range(count)
    ]
    seg_all = lax.dynamic_index_in_dim(small, section, 0, False)[:, cuts[6] : cuts[7]]
    seg_near = jnp.take(seg_all, table_row(table, "fsdp"), axis=0)
    tables = [block_tables(seg_near[2 * spot : 2 * spot + 2]) for spot in range(len(groups))]

    layer_in = lax.dynamic_index_in_dim(inputs, section, 0, False)
    first_out, first_store = layer_forward(layer_in, tables, layers[0])
    second_out, second_store = layer_forward(first_out, tables, layers[1])
    grad = lax.dynamic_index_in_dim(cotangent, section, 0, False)
    second_grad, g_in_1, g_out_1, sums_1, tokens_1 = layer_backward(
        grad, tables, second_store, layers[1]
    )
    first_grad, g_in_0, g_out_0, sums_0, tokens_0 = layer_backward(
        second_grad, tables, first_store, layers[0]
    )

    def across(first, second):
        to_first = one_way(first, "section", 1)
        to_second = one_way(second, "section", 0)
        return jnp.where(
            first_plane, jnp.stack([first, to_first]), jnp.stack([to_second, second])
        )[None]

    layer_out = across(first_out, second_out)
    input_grad = across(first_grad, second_grad)

    def core_half(value, axis):
        size = value.shape[axis] // 2
        mine = lax.dynamic_slice_in_dim(value, core * size, size, axis)
        theirs = lax.dynamic_slice_in_dim(value, (1 - core) * size, size, axis)
        return (mine.astype(F32) + swap(theirs, "rep").astype(F32)).astype(BF16)

    def plane_sum(first, second):
        from_other = jnp.where(
            first_plane, one_way(first, "section", 1), one_way(second, "section", 0)
        )
        own = jnp.where(first_plane, first, second)
        return (own.astype(F32) + from_other.astype(F32)).astype(BF16)

    def sum_parts(g_in, g_out):
        qkv = core_half(g_in[: 3 * unit].reshape(3, unit, width), 1)
        up = core_half(g_in[3 * unit :], 0)
        out = core_half(g_out.reshape(count, out_rows, features), 1)
        return qkv, up, out

    qkv_1, up_1, out_1 = sum_parts(g_in_1, g_out_1)
    qkv_0, up_0, out_0 = sum_parts(g_in_0, g_out_0)
    out_half = exchange(plane_sum(out_0, out_1))
    qkv_half = heads_to_units(plane_sum(qkv_0, qkv_1))
    up_half = plane_sum(up_0, up_1)
    out_all = halves(out_half, swap(out_half, "rep"), second_core, 1).astype(F32)
    g_w_dense = out_all[:, :, :unit].transpose(1, 0, 2).reshape(out_rows, count * unit)
    g_w_down = out_all[:, :, unit:].transpose(1, 0, 2).reshape(out_rows, count * up_units)
    g_w_qkv = halves(qkv_half, swap(qkv_half, "rep"), second_core, 1).astype(F32)
    g_w_qkv = g_w_qkv.reshape(3 * unit, width)
    g_w_up = halves(up_half, swap(up_half, "rep"), second_core, 0).astype(F32)

    def spread(sums, tokens):
        qkv = lax.dynamic_update_slice(
            jnp.zeros((3, count, unit), F32), sums[: 3 * unit].reshape(3, 1, unit), (0, place, 0)
        )
        up = lax.dynamic_update_slice(
            jnp.zeros((count, up_units), F32), sums[3 * unit :].reshape(1, up_units), (place, 0)
        )
        return jnp.concatenate([qkv.reshape(-1), up.reshape(-1), tokens.reshape(-1)])

    vectors = lax.psum(
        jnp.stack([spread(sums_0, tokens_0), spread(sums_1, tokens_1)]),
        ("section", "rep", "fsdp"),
    )
    vectors = lax.dynamic_index_in_dim(vectors, section, 0, False)
    cut = 3 * unit * count

    def own_part(start, size):
        return lax.dynamic_slice_in_dim(vectors, start + place * size, size, 0)

    g_b_qkv = own_part(0, 3 * unit)
    g_b_up = own_part(cut, up_units)
    cut = cut + up_units * count
    g_b_dense = own_part(cut, out_rows)
    g_gain = own_part(cut + width, out_rows)
    g_bias = own_part(cut + 2 * width, out_rows)
    grads = (
        g_w_qkv,
        g_b_qkv,
        g_w_dense,
        g_b_dense,
        g_w_up,
        g_b_up,
        g_w_down,
        g_b_dense,
        g_gain,
        g_bias,
    )
    return (layer_out, input_grad) + tuple(member[None] for member in grads)


def solution(mesh):
    in_specs = (
        P(None, ("rep", "fsdp"), None),
        P(None, ("rep", "fsdp")),
        P(None, ("rep", "fsdp"), None),
        P("section", "fsdp", None),
        P("section", "fsdp"),
        P("section", "fsdp", None),
        P("section", "fsdp"),
        P("section", "fsdp", None),
        P("section", "fsdp"),
        P("section", "fsdp", None),
        P("section", "fsdp"),
        P("section", "fsdp"),
        P("section", "fsdp"),
    )
    out_specs = (
        P("section", None, ("rep", "fsdp"), None),
        P("section", None, ("rep", "fsdp"), None),
        P("section", "fsdp", None),
        P("section", "fsdp"),
        P("section", "fsdp", None),
        P("section", "fsdp"),
        P("section", "fsdp", None),
        P("section", "fsdp"),
        P("section", "fsdp", None),
        P("section", "fsdp"),
        P("section", "fsdp"),
        P("section", "fsdp"),
    )
    return jax.shard_map(shards, mesh=mesh, in_specs=in_specs, out_specs=out_specs, check_vma=False)
```
